32 devices in a mesh: gx: 16 (over z, y, core), gy: 2 (over x).
Axes of the slice: x: 2, y: 2, z: 4, core: 2. Of those that a mesh axis runs over, the one named last changes fastest.
Arguments:
- velocity: float32 [3, 256, 32, 128], P(None, 'gx', 'gy'), may hold values from -6 to 6
- pressure: float32 [256, 32, 128], P('gx', 'gy'), may hold values from -6 to 6
- land_type: int32 [256, 32], P('gx', 'gy'), may hold values from 0 to 15
- turbine_cells: int32 [256, 32, 128], P('gx', 'gy'), may hold values 0 or 1
- surface_drag: float32 [16], replicated, may hold values from 0.2 to 2
Outputs:
- velocity_new: float32 [3, 256, 32, 128], P(None, 'gx', 'gy')
- pressure_new: float32 [256, 32, 128], P('gx', 'gy')
The draws below stay inside these ranges and needn't reach their ends.
All inputs are finite; a program needn't handle non-finite values. No bound on the sum of `turbine_cells` on one device may be relied on, other than what follows from the above.
Results may differ from the reference program's by a relative error of at most 0.00002.
Values sent between devices are 32-bit elements; how exact they have to be, the bound alone decides.
A program may use at most 64 MiB of HBM per device.

```python
import math
import jax
import jax.numpy as jnp
from jax import lax

NZ = 128
TYPES = 16
SWEEPS = 2
COARSE_SWEEPS = 4
NX = 256
NY = 32


def set_ends(result, rng, low, top_value):
    spot = [jax.random.randint(jax.random.fold_in(rng, axis), (), 0, length) for axis, length in enumerate(result.shape)]
    main_axis = result.shape.index(max(result.shape))
    neighbour = spot[:main_axis] + [(spot[main_axis] + 1) % result.shape[main_axis]] + spot[main_axis + 1:]
    return result.at[tuple(spot)].set(low).at[tuple(neighbour)].set(top_value)


def shard_levels(own_key, shape, shards, low, high):
    def one(position, blocks):
        heights = jax.random.uniform(jax.random.fold_in(jax.random.fold_in(own_key, 6), position), (blocks,), jnp.float32, low / len(shards), high / len(shards))
        return jnp.repeat(jnp.exp(heights), shape[position] // blocks).reshape((-1,) + (1,) * (len(shape) - position - 1))

    factor_of = one(*shards[0])
    for cut in shards[1:]:
        factor_of = factor_of * one(*cut)
    return factor_of


def centred(stream_key, extent, width, reach, split=(), held_as=jnp.bfloat16):
    result = width * jax.random.normal(stream_key, extent, jnp.float32)
    if split:
        result = result * shard_levels(stream_key, extent, split, -0.22, 0.18)
    return jnp.clip(result, -reach, reach).astype(held_as)


def setup_inputs(seed: int = 0) -> dict:
    arg_keys = jax.random.split(jax.random.key(seed), 6)
    return {
        "velocity": centred(arg_keys[0], (3, NX, NY, NZ), 1.0, 6.0, ((1, 16), (2, 2)), jnp.float32),
        "pressure": centred(arg_keys[1], (NX, NY, NZ), 1.0, 6.0, ((0, 16), (1, 2)), jnp.float32),
        "land_type": set_ends(jax.random.randint(arg_keys[2], (NX, NY), 0, TYPES), jax.random.fold_in(arg_keys[2], 1), 0, TYPES - 1).astype(jnp.int32),
        "turbine_cells": set_ends((jax.random.randint(arg_keys[3], (NX, NY, NZ), 0, 8) < 1).astype(jnp.int32), jax.random.fold_in(arg_keys[3], 1), 0, 1),
        "surface_drag": jnp.clip(jnp.exp(jax.random.uniform(arg_keys[4], (TYPES,), jnp.float32, math.log(0.2), math.log(2.0))), 0.2, 2.0),
    }


time_step = 0.1
vertical_step = 0.5
eddy_coeff = 0.03
thrust_factor = 2.0
relax_weight = 0.8
driving_force = 1.0

def shifted(values, axis_pos, offset):
    starts = [1, 1, 1]
    starts[axis_pos] = 1 + offset
    length = [values.shape[-3] - 2, values.shape[-2] - 2, values.shape[-1] - 2]
    return values[..., starts[0]:starts[0] + length[0], starts[1]:starts[1] + length[1], starts[2]:starts[2] + length[2]]

def central(values, axis_pos):
    spacing = vertical_step if axis_pos == 2 else 1.0
    return (shifted(values, axis_pos, 1) - shifted(values, axis_pos, -1)) * (0.5 / spacing)

def surface_field(land_type, turbine_cells, surface_drag):
    kind_ids = jnp.arange(surface_drag.shape[0], dtype=jnp.int32)
    ground = lax.optimization_barrier(jnp.sum(jnp.where(land_type[:, :, None] == kind_ids, surface_drag, 0.0), axis=-1))
    ground_layer = jnp.arange(turbine_cells.shape[2], dtype=jnp.int32) == 0
    return thrust_factor * turbine_cells.astype(jnp.float32) + jnp.where(ground_layer, ground[:, :, None], 0.0)

def advance(padded, drag_field):
    gradient = [central(padded, axis_pos) for axis_pos in range(3)]
    strain = [[0.5 * (gradient[col_idx][row_idx] + gradient[row_idx][col_idx]) for col_idx in range(3)] for row_idx in range(3)]
    square_sum = strain[0][0] * strain[0][0]
    for row_idx in range(3):
        for col_idx in range(3):
            if row_idx + col_idx > 0:
                square_sum = square_sum + strain[row_idx][col_idx] * strain[row_idx][col_idx]
    viscosity = eddy_coeff * jnp.sqrt(2.0 * square_sum)
    centre = padded[:, 2:-2, 2:-2, 2:-2]
    wind_speed = jnp.sqrt(centre[0] * centre[0] + centre[1] * centre[1])
    updated = []
    for row_idx in range(3):
        change = jnp.zeros_like(centre[0])
        for col_idx in range(3):
            stress = 2.0 * viscosity * strain[row_idx][col_idx]
            change = change + central(stress, col_idx) - centre[col_idx] * gradient[col_idx][row_idx][1:-1, 1:-1, 1:-1]
        if row_idx < 2:
            change = change - drag_field * wind_speed * centre[row_idx]
        if row_idx == 0:
            change = change + driving_force
        updated.append(centre[row_idx] + time_step * change)
    return jnp.stack(updated)

def divergence(padded):
    return central(padded[0], 0) + central(padded[1], 1) + central(padded[2], 2)

def laplace(padded, spacing):
    centre = padded[1:-1, 1:-1, 1:-1]
    upright = vertical_step * spacing
    horizontal = (shifted(padded, 0, 1) + shifted(padded, 0, -1) + shifted(padded, 1, 1) + shifted(padded, 1, -1) - 4.0 * centre) / (spacing * spacing)
    vertical = (shifted(padded, 2, 1) + shifted(padded, 2, -1) - 2.0 * centre) / (upright * upright)
    return horizontal + vertical

def diagonal_of(spacing):
    upright = vertical_step * spacing
    return -(4.0 / (spacing * spacing) + 2.0 / (upright * upright))

def relax(pressure, padded, source, spacing):
    return pressure + relax_weight * (source - laplace(padded, spacing)) / diagonal_of(spacing)

def line_correct(pressure, residual, spacing):
    return pressure + relax_weight * lax.optimization_barrier(jnp.mean(residual, axis=1, keepdims=True)) / diagonal_of(spacing)

def periodic(values, pad_width, vertical_mode):
    leading = [(0, 0)] * (values.ndim - 3)
    values = jnp.pad(values, leading + [(pad_width, pad_width), (pad_width, pad_width), (0, 0)], mode='wrap')
    return jnp.pad(values, leading + [(0, 0), (0, 0), (pad_width, pad_width)], mode=vertical_mode)

def coarsen(values):
    return values.reshape(values.shape[0] // 2, 2, values.shape[1] // 2, 2, values.shape[2] // 2, 2).mean(axis=(1, 3, 5))

def refine(values):
    return jnp.repeat(jnp.repeat(jnp.repeat(values, 2, axis=0), 2, axis=1), 2, axis=2)

def cycle(pressure, source, depth_level):
    spacing = 2.0 ** depth_level
    if depth_level == 3:
        for sweep_idx in range(COARSE_SWEEPS):
            pressure = relax(pressure, periodic(pressure, 1, 'edge'), source, spacing)
        residual = source - laplace(periodic(pressure, 1, 'edge'), spacing)
        return line_correct(pressure, residual, spacing)
    for sweep_idx in range(SWEEPS):
        pressure = relax(pressure, periodic(pressure, 1, 'edge'), source, spacing)
    residual = source - laplace(periodic(pressure, 1, 'edge'), spacing)
    coarse_source = coarsen(residual)
    correction = cycle(jnp.zeros_like(coarse_source), coarse_source, depth_level + 1)
    pressure = pressure + refine(correction)
    for sweep_idx in range(SWEEPS):
        pressure = relax(pressure, periodic(pressure, 1, 'edge'), source, spacing)
    return pressure

def reference(velocity, pressure, land_type, turbine_cells, surface_drag):
    drag_field = surface_field(land_type, turbine_cells, surface_drag)
    star_velocity = advance(periodic(velocity, 2, 'constant'), drag_field)
    source = divergence(periodic(star_velocity, 1, 'constant')) / time_step
    pressure_new = cycle(pressure, source, 0)
    padded = periodic(pressure_new, 1, 'edge')
    gradient = jnp.stack([central(padded, 0), central(padded, 1), central(padded, 2)])
    return (star_velocity - time_step * gradient, pressure_new)
```

```python
import functools

import jax
import jax.numpy as jnp
from jax import lax
from jax.experimental import pallas as pl
from jax.experimental.pallas import tpu as pltpu
from jax.sharding import PartitionSpec as P

MESH = pl.DeviceIdType.MESH
F32 = jnp.float32
STEP = 0.1
WEIGHT = 0.8 / 12.0
KEEP = 0.2
OFF = 3
REACH = 4


def loop(low, high, body):
    def step(index, carry):
        body(index)
        return carry

    lax.fori_loop(low, high, step, 0)


def kernel(
    nx, ny, vel_in, pre_in, turb_in, ground_in, vel_out, pre_out,
    W, WLO, WHI, WSL, WSH, D, DLO, DHI, DSL, DSH, PA, PLO, PHI, PSL, PSH,
    PB, PC, CLO, CHI, CSL, CSH, F, FLO, FHI, FSL, FSH, T, S, tmp, tmp2, turb, ground,
    G1, F1, P1A, P1B, G2, F2, P2A, P2B, F3, P3A, P3B, E1, E0,
    load_sem, send_sem, recv_sem,
):
    me_x, me_y = lax.axis_index("gx"), lax.axis_index("gy")
    own_x, own_y, nz = pre_out.shape
    side = (own_y // 8 + 1) * 8
    rows = own_x + 2 * OFF

    loads = [
        pltpu.make_async_copy(vel_in, W.at[:, OFF : OFF + own_x, 0:own_y], load_sem.at[0]),
        pltpu.make_async_copy(pre_in, PA.at[OFF : OFF + own_x, 0:own_y], load_sem.at[1]),
        pltpu.make_async_copy(turb_in, turb, load_sem.at[2]),
        pltpu.make_async_copy(ground_in, ground, load_sem.at[3]),
    ]
    for load in loads:
        load.start()

    def device(dx, dy):
        return (lax.rem(me_x + dx + nx, nx), lax.rem(me_y + dy + ny, ny))

    friends = [(dx, 0) for dx in range(-REACH, REACH + 1) if dx != 0]
    friends += [(dx, dy) for dx in (-1, 0, 1) for dy in range(1, ny)]
    barrier = pltpu.get_barrier_semaphore()
    for dx, dy in friends:
        pl.semaphore_signal(barrier, inc=1, device_id=device(dx, dy), device_id_type=MESH)

    used = [0]

    def remote(src, dst, where):
        slot = used[0]
        used[0] += 1
        copy = pltpu.make_async_remote_copy(
            src_ref=src, dst_ref=dst, send_sem=send_sem.at[slot], recv_sem=recv_sem.at[slot],
            device_id=where, device_id_type=MESH,
        )
        copy.start()
        return copy

    def spans(dx, width, base):
        if dx == 0:
            return pl.ds(base, own_x), pl.ds(base, own_x)
        if dx == 1:
            return pl.ds(base + own_x - width, width), pl.ds(base - width, width)
        return pl.ds(base, width), pl.ds(base + own_x, width)

    def pick(ref, span, lead):
        return ref.at[:, span] if lead else ref.at[span]

    def send_x(M, width, lead=False):
        copies = []
        for dx in (1, -1):
            src, dst = spans(dx, width, OFF)
            a = M.at[:, src, 0:own_y] if lead else M.at[src, 0:own_y]
            b = M.at[:, dst, 0:own_y] if lead else M.at[dst, 0:own_y]
            copies.append(remote(a, b, device(dx, 0)))
        return copies

    def send_y(M, LO, HI, SL, SH, width, lead=False):
        if lead:
            SL[...] = M[:, OFF : OFF + own_x, own_y - width : own_y, :]
            SH[...] = M[:, OFF : OFF + own_x, 0:width, :]
        else:
            SL[...] = M[OFF : OFF + own_x, own_y - width : own_y, :]
            SH[...] = M[OFF : OFF + own_x, 0:width, :]
        copies = []
        for dx in (0, 1, -1):
            src, dst = spans(dx, width, width)
            if dx == 0:
                src = pl.ds(0, own_x)
            elif dx == 1:
                src = pl.ds(own_x - width, width)
            else:
                src = pl.ds(0, width)
            copies.append(remote(pick(SL, src, lead), pick(LO, dst, lead), device(dx, 1)))
            copies.append(remote(pick(SH, src, lead), pick(HI, dst, lead), device(dx, -1)))
        return copies

    def finish(copies):
        for copy in copies:
            copy.wait()

    def place(M, LO, HI, width, lead=False):
        lo, hi = OFF - width, OFF + own_x + width
        if lead:
            M[:, lo:hi, own_y : own_y + width, :] = HI[...]
            M[:, lo:hi, side - width : side, :] = LO[...]
        else:
            M[lo:hi, own_y : own_y + width, :] = HI[...]
            M[lo:hi, side - width : side, :] = LO[...]

    def lane_of(count):
        return lax.broadcasted_iota(jnp.int32, (count, nz), 1)

    def roll(v, shift, axis):
        return pltpu.roll(v, shift % v.shape[axis], axis)

    lane16 = lane_of(own_y)
    loads[2].wait()
    loads[3].wait()
    for x in range(own_x):
        low = jnp.where(lane16 == 0, roll(ground[...], -x, 1), 0.0)
        D[OFF + x, 0:own_y, :] = 2.0 * turb[x].astype(F32) + low
    loads[0].wait()
    loads[1].wait()
    pl.semaphore_wait(barrier, len(friends))
    w_copies = send_y(W, WLO, WHI, WSL, WSH, 3, True) + send_x(W, 3, True)
    d_copies = send_y(D, DLO, DHI, DSL, DSH, 1) + send_x(D, 1)
    p_copies = send_y(PA, PLO, PHI, PSL, PSH, 3) + send_x(PA, 3)
    finish(w_copies)
    place(W, WLO, WHI, 3, True)
    finish(d_copies)
    place(D, DLO, DHI, 1)

    lane = lane_of(side)
    first, last = lane == 0, lane == nz - 1

    def up0(v):
        return jnp.where(last, 0.0, roll(v, -1, 1))

    def down0(v):
        return jnp.where(first, 0.0, roll(v, 1, 1))

    def stress_row(r):
        v = [W[a, r] for a in range(3)]
        gx = [0.5 * (W[a, r + 1] - W[a, r - 1]) for a in range(3)]
        gy = [0.5 * (roll(v[a], -1, 0) - roll(v[a], 1, 0)) for a in range(3)]
        gz = [up0(v[a]) - down0(v[a]) for a in range(3)]
        e01, e02, e12 = gx[1] + gy[0], gx[2] + gz[0], gy[2] + gz[1]
        q = 2.0 * (gx[0] * gx[0] + gy[1] * gy[1] + gz[2] * gz[2]) + e01 * e01 + e02 * e02 + e12 * e12
        visc = 0.03 * jnp.sqrt(q)
        twice = visc + visc
        t00, t11, t22 = twice * gx[0], twice * gy[1], twice * gz[2]
        t01, t02, t12 = visc * e01, visc * e02, visc * e12
        flat = v[0] * v[0] + v[1] * v[1]
        ghost = 0.03 * jnp.sqrt(2.0 * v[2] * v[2] + flat)
        ghosts = [ghost * v[0], ghost * v[1], (ghost + ghost) * v[2]]
        T[0, r] = t00
        T[1, r] = t01
        T[2, r] = t02
        drag = D[r] * jnp.sqrt(flat)
        for a, (ty, tz) in enumerate(((t01, t02), (t11, t12), (t12, t22))):
            change = 0.5 * (roll(ty, -1, 0) - roll(ty, 1, 0))
            change += jnp.where(last, -ghosts[a], roll(tz, -1, 1)) - jnp.where(first, ghosts[a], roll(tz, 1, 1))
            change -= v[0] * gx[a] + v[1] * gy[a] + v[2] * gz[a]
            if a < 2:
                change -= drag * v[a]
            if a == 0:
                change += 1.0
            S[a, r] = v[a] + STEP * change

    loop(1, rows - 1, stress_row)

    def star_row(r):
        for a in range(3):
            S[a, r] = S[a, r] + (0.5 * STEP) * (T[a, r + 1] - T[a, r - 1])

    loop(2, rows - 2, star_row)

    def source_row(r):
        s1, s2 = S[1, r], S[2, r]
        flat = 0.5 * (S[0, r + 1] - S[0, r - 1] + roll(s1, -1, 0) - roll(s1, 1, 0))
        F[r] = (flat + up0(s2) - down0(s2)) / STEP

    loop(OFF, OFF + own_x, source_row)
    f_copies = send_y(F, FLO, FHI, FSL, FSH, 2) + send_x(F, 2)
    finish(p_copies)
    place(PA, PLO, PHI, 3)
    finish(f_copies)
    place(F, FLO, FHI, 2)

    def stencil(src, r, sy, sz):
        p = src[r]
        lanes = lane_of(p.shape[0])
        z = jnp.where(lanes >= nz - sz, p, roll(p, -sz, 1)) + jnp.where(lanes < sz, p, roll(p, sz, 1))
        s = src[r + 1] + src[r - 1] + roll(p, -sy, 0) + roll(p, sy, 0)
        return p, s + 4.0 * z

    def sweep(src, dst, f, low, high, sy, sz):
        def body(r):
            p, around = stencil(src, r, sy, sz)
            dst[r] = KEEP * p + WEIGHT * (around - f[r])

        loop(low, high, body)

    def residual(src, f, r, sy, sz):
        p, around = stencil(src, r, sy, sz)
        return f[r] - (around - 12.0 * p)

    def pair(v, stride, axis):
        at = lax.broadcasted_iota(jnp.int32, v.shape, axis)
        even = (at // stride) % 2 == 0
        return v + jnp.where(even, roll(v, -stride, axis), roll(v, stride, axis))

    def spread(v, stride, bit):
        at = (lane_of(v.shape[0]) // stride) % 2
        return jnp.where(at == bit, v, roll(v, stride if bit == 0 else -stride, 1))

    sweep(PA, PB, F, 1, rows - 1, 1, 1)
    sweep(PB, PA, F, 2, rows - 2, 1, 1)
    PC[OFF : OFF + own_x, 0:own_y, :] = PA[OFF : OFF + own_x, 0:own_y, :]

    half = own_x // 2
    y1 = own_y // 2

    def fine_residual(i):
        r = OFF + 2 * i
        v = residual(PA, F, r, 1, 1) + residual(PA, F, r + 1, 1, 1)
        tmp[i] = pair(v[0:own_y], 1, 1)

    loop(0, half, fine_residual)
    packed = half // 2
    lane8 = lane_of(y1)
    for i in range(packed):
        parts = []
        for x in (2 * i, 2 * i + 1):
            parts.append(0.5 * (tmp[x, pl.ds(0, y1, 2), :] + tmp[x, pl.ds(1, y1, 2), :]))
        G1[0, 3 + i] = jnp.where(lane8 % 2 == 0, parts[0], parts[1])
    g_copies = []
    for dx in (1, -1, 0):
        for dy in range(ny):
            if dx == 0 and dy == 0:
                continue
            if dx == 0:
                src, dst = pl.ds(3, packed), pl.ds(3, packed)
            elif dx == 1:
                src, dst = pl.ds(packed, 3), pl.ds(0, 3)
            else:
                src, dst = pl.ds(3, 3), pl.ds(3 + packed, 3)
            g_copies.append(remote(G1.at[0, src], G1.at[(ny - dy) % ny, dst], device(dx, dy)))
    c_copies = send_y(PC, CLO, CHI, CSL, CSH, 3) + send_x(PC, 3)
    finish(g_copies)
    rows1 = 2 * (packed + 6)
    for k in range(ny):
        for j in range(packed + 6):
            v = G1[k, j]
            for bit in (0, 1):
                f = spread(v, 1, bit)
                F1[2 * j + bit, k * y1 : (k + 1) * y1, :] = f
                P1A[2 * j + bit, k * y1 : (k + 1) * y1, :] = -WEIGHT * f
    sweep(P1A, P1B, F1, 1, rows1 - 1, 1, 2)
    quarter = half // 2
    y2 = ny * y1 // 2
    lane2 = lane_of(y2)
    gathered = None
    for i in range(quarter):
        r = 6 + 2 * i
        tmp2[i] = pair(residual(P1B, F1, r, 1, 2) + residual(P1B, F1, r + 1, 1, 2), 2, 1)
        v = 0.5 * (tmp2[i, pl.ds(0, y2, 2), :] + tmp2[i, pl.ds(1, y2, 2), :])
        gathered = v if gathered is None else jnp.where(lane2 % 4 == i, v, gathered)
    G2[REACH] = gathered
    finish([remote(G2.at[REACH], G2.at[REACH - dx], device(dx, 0)) for dx, dy in friends if dy == 0])
    for s in range(2 * REACH + 1):
        v = G2[s]
        for b0 in (0, 1):
            u = spread(v, 1, b0)
            for b1 in (0, 1):
                f = spread(u, 2, b1)
                F2[4 * s + 2 * b1 + b0] = f
                P2A[4 * s + 2 * b1 + b0] = -WEIGHT * f
    rows2 = 4 * (2 * REACH + 1)
    sweep(P2A, P2B, F2, 1, rows2 - 1, 1, 4)

    def coarse_source(i):
        v = residual(P2B, F2, 2 * i, 1, 4) + residual(P2B, F2, 2 * i + 1, 1, 4)
        f = 0.5 * pair(pair(v, 4, 1), 1, 0)
        F3[i] = f
        P3A[i] = -WEIGHT * f

    loop(1, rows2 // 2 - 1, coarse_source)
    sweep(P3A, P3B, F3, 2, 16, 2, 8)
    sweep(P3B, P3A, F3, 3, 15, 2, 8)
    sweep(P3A, P3B, F3, 4, 14, 2, 8)

    def line_row(r):
        mean = jnp.mean(residual(P3B, F3, r, 2, 8), axis=0, keepdims=True)
        v = P3B[r] - WEIGHT * mean
        P2B[2 * r] = P2B[2 * r] + v
        P2B[2 * r + 1] = P2B[2 * r + 1] + v

    loop(6, 12, line_row)
    sweep(P2B, P2A, F2, 13, 23, 1, 4)

    def second_row(m):
        p, around = stencil(P2A, m, 1, 4)
        v = KEEP * p + WEIGHT * (around - F2[m])
        E1[m - 14, pl.ds(0, y2, 2), :] = v
        E1[m - 14, pl.ds(1, y2, 2), :] = v
        e = E1[m - 14]
        r = 2 * (m - 13)
        P1B[r] = P1B[r] + e
        P1B[r + 1] = P1B[r + 1] + e

    for m in range(14, 22):
        second_row(m)
    sweep(P1B, P1A, F1, 3, 17, 1, 2)
    sweep(P1A, P1B, F1, 4, 16, 1, 2)
    finish(c_copies)
    place(PC, CLO, CHI, 3)
    full1 = ny * y1
    for m in range(4, 16):
        e = m - 4
        for shift in (0, 1):
            E0[e, pl.ds(shift, y1, 2), :] = P1B[m, 0:y1, :]
            E0[e, pl.ds(own_y + shift, 2, 2), :] = P1B[m, y1 : y1 + 2, :]
            E0[e, pl.ds(own_y + 4 + shift, 2, 2), :] = P1B[m, full1 - 2 : full1, :]
        for r in (2 * m - 9, 2 * m - 8):
            if 0 <= r < rows:
                PC[r] = PC[r] + E0[e]
    sweep(PC, PA, F, 1, rows - 1, 1, 1)
    sweep(PA, PB, F, 2, rows - 2, 1, 1)

    def out_row(x):
        r = OFF + x
        p = PB[r]
        pre_out[x] = p[0:own_y]
        gx = (0.5 * STEP) * (PB[r + 1] - PB[r - 1])
        gy = (0.5 * STEP) * (roll(p, -1, 0) - roll(p, 1, 0))
        gz = STEP * (jnp.where(last, p, roll(p, -1, 1)) - jnp.where(first, p, roll(p, 1, 1)))
        for a, g in enumerate((gx, gy, gz)):
            vel_out[a, x] = (S[a, r] - g)[0:own_y]

    loop(0, own_x, out_row)


def per_device(nx, ny, velocity, pressure, land_type, turbine_cells, surface_drag):
    _, own_x, own_y, nz = velocity.shape
    kinds = jnp.arange(surface_drag.shape[0], dtype=jnp.int32)
    ground = jnp.sum(jnp.where(land_type.T[:, :, None] == kinds, surface_drag, 0.0), axis=-1)
    ground = jnp.pad(ground, ((0, 0), (0, nz - own_x)))
    side = (own_y // 8 + 1) * 8
    rows = own_x + 2 * OFF
    window = pltpu.VMEM((rows, side, nz), F32)

    def rims(width, *lead):
        rim = pltpu.VMEM((*lead, own_x + 2 * width, width, nz), F32)
        stage = pltpu.VMEM((*lead, own_x, width, nz), F32)
        return [rim, rim, stage, stage]

    three = pltpu.VMEM((3, rows, side, nz), F32)
    half, quarter = own_x // 2, own_x // 4
    y1 = own_y // 2
    full1, full2 = ny * y1, ny * y1 // 2
    packed = half // 2
    level1 = pltpu.VMEM((2 * (packed + 6), full1, nz), F32)
    rows2 = quarter * (2 * REACH + 1)
    level2 = pltpu.VMEM((rows2, full2, nz), F32)
    level3 = pltpu.VMEM((rows2 // 2, full2, nz), F32)
    count = 5 * 8 + 3 * ny - 1 + 2 * REACH
    scratch = [three] + rims(3, 3) + [window] + rims(1) + [window] + rims(3)
    scratch += [window, window] + rims(3) + [window] + rims(2) + [three, three]
    scratch += [
        pltpu.VMEM((half, own_y, nz), F32),
        pltpu.VMEM((quarter, full1, nz), F32),
        pltpu.VMEM((own_x, own_y, nz), jnp.int32),
        pltpu.VMEM((own_y, nz), F32),
        pltpu.VMEM((ny, packed + 6, y1, nz), F32),
        level1, level1, level1,
        pltpu.VMEM((2 * REACH + 1, full2, nz), F32),
        level2, level2, level2, level3, level3, level3,
        pltpu.VMEM((8, full1, nz), F32),
        pltpu.VMEM((12, side, nz), F32),
        pltpu.SemaphoreType.DMA((4,)),
        pltpu.SemaphoreType.DMA((count,)),
        pltpu.SemaphoreType.DMA((count,)),
    ]
    anywhere = pl.BlockSpec(memory_space=pl.ANY)
    inside = pl.BlockSpec(memory_space=pltpu.VMEM)
    return tuple(
        pl.pallas_call(
            functools.partial(kernel, nx, ny),
            out_shape=(
                jax.ShapeDtypeStruct(velocity.shape, F32),
                jax.ShapeDtypeStruct(pressure.shape, F32),
            ),
            in_specs=[anywhere] * 4,
            out_specs=(inside, inside),
            scratch_shapes=scratch,
            compiler_params=pltpu.CompilerParams(collective_id=0, has_side_effects=True),
        )(velocity, pressure, turbine_cells, ground)
    )


def solution(mesh):
    in_specs = (
        P(None, "gx", "gy", None),
        P("gx", "gy", None),
        P("gx", "gy"),
        P("gx", "gy", None),
        P(),
    )
    out_specs = (P(None, "gx", "gy", None), P("gx", "gy", None))
    body = functools.partial(per_device, mesh.shape["gx"], mesh.shape["gy"])
    return jax.shard_map(
        body, mesh=mesh, in_specs=in_specs, out_specs=out_specs, check_vma=False
    )
```

```python
import functools

import jax
import jax.numpy as jnp
from jax import lax
from jax.experimental import pallas as pl
from jax.experimental.pallas import tpu as pltpu
from jax.sharding import PartitionSpec as P

MESH = pl.DeviceIdType.MESH
F32 = jnp.float32
STEP = 0.1
WEIGHT = 0.8 / 12.0
KEEP = 0.2
OFF = 3
G_STRESS = 4
G_FINE = 8
VMEM_LIMIT = 60 * 1024 * 1024
REACH = 4


def loop(low, high, body, group):
    def run(indices):
        found = [store for index in indices for store in body(index)]
        for ref, at, value in found:
            ref[at] = value

    whole = (high - low) // group
    if whole == 1:
        run(range(low, low + group))
    elif whole > 1:

        def step(index, carry):
            run([low + index * group + k for k in range(group)])
            return carry

        lax.fori_loop(0, whole, step, 0)
    if low + whole * group < high:
        run(range(low + whole * group, high))


def kernel(
    nx, ny, vel_in, pre_in, turb_in, land_in, coeff_in, vel_out, pre_out,
    W, WLO, WHI, WSL, WSH, D, DLO, DHI, DSL, DSH, PA, PLO, PHI, PSL, PSH,
    PB, PC, CLO, CHI, CSL, CSH, F, FLO, FHI, FSL, FSH, T, S, tmp, tmp2, turb, land, coeff,
    G1, F1, P1A, P1B, G2, F2, P2A, P2B, F3, P3A, P3B, E1, E0,
    load_sem, send_sem, recv_sem,
):
    me_x, me_y = lax.axis_index("gx"), lax.axis_index("gy")
    own_x, own_y, nz = pre_out.shape
    side = (own_y // 8 + 1) * 8
    rows = own_x + 2 * OFF

    loads = [
        pltpu.make_async_copy(vel_in, W.at[:, OFF : OFF + own_x, 0:own_y], load_sem.at[0]),
        pltpu.make_async_copy(pre_in, PA.at[OFF : OFF + own_x, 0:own_y], load_sem.at[1]),
        pltpu.make_async_copy(turb_in, turb, load_sem.at[2]),
        pltpu.make_async_copy(land_in, land, load_sem.at[3]),
        pltpu.make_async_copy(coeff_in, coeff, load_sem.at[4]),
    ]
    for load in loads:
        load.start()

    def device(dx, dy):
        return (lax.rem(me_x + dx + nx, nx), lax.rem(me_y + dy + ny, ny))

    friends = [(dx, 0) for dx in range(-REACH, REACH + 1) if dx != 0]
    friends += [(dx, dy) for dx in (-1, 0, 1) for dy in range(1, ny)]
    close = [(dx, dy) for dx, dy in friends if abs(dx) < 2]
    barrier = pltpu.get_barrier_semaphore()
    for dx, dy in close:
        pl.semaphore_signal(barrier, inc=1, device_id=device(dx, dy), device_id_type=MESH)

    used = [0]

    def remote(src, dst, where):
        slot = used[0]
        used[0] += 1
        copy = pltpu.make_async_remote_copy(
            src_ref=src, dst_ref=dst, send_sem=send_sem.at[slot], recv_sem=recv_sem.at[slot],
            device_id=where, device_id_type=MESH,
        )
        copy.start()
        return copy

    def spans(dx, width, base):
        if dx == 0:
            return pl.ds(base, own_x), pl.ds(base, own_x)
        if dx == 1:
            return pl.ds(base + own_x - width, width), pl.ds(base - width, width)
        return pl.ds(base, width), pl.ds(base + own_x, width)

    def pick(ref, span, lead):
        return ref.at[:, span] if lead else ref.at[span]

    def send_x(M, width, lead=False):
        copies = []
        for dx in (1, -1):
            src, dst = spans(dx, width, OFF)
            a = M.at[:, src, 0:own_y] if lead else M.at[src, 0:own_y]
            b = M.at[:, dst, 0:own_y] if lead else M.at[dst, 0:own_y]
            copies.append(remote(a, b, device(dx, 0)))
        return copies

    def send_y(M, LO, HI, SL, SH, width, lead=False):
        if lead:
            SL[...] = M[:, OFF : OFF + own_x, own_y - width : own_y, :]
            SH[...] = M[:, OFF : OFF + own_x, 0:width, :]
        else:
            SL[...] = M[OFF : OFF + own_x, own_y - width : own_y, :]
            SH[...] = M[OFF : OFF + own_x, 0:width, :]
        copies = []
        for dx in (0, 1, -1):
            src, dst = spans(dx, width, width)
            if dx == 0:
                src = pl.ds(0, own_x)
            elif dx == 1:
                src = pl.ds(own_x - width, width)
            else:
                src = pl.ds(0, width)
            copies.append(remote(pick(SL, src, lead), pick(LO, dst, lead), device(dx, 1)))
            copies.append(remote(pick(SH, src, lead), pick(HI, dst, lead), device(dx, -1)))
        return copies

    def finish(copies):
        for copy in copies:
            copy.wait()

    def place(M, LO, HI, width, lead=False):
        lo, hi = OFF - width, OFF + own_x + width
        if lead:
            M[:, lo:hi, own_y : own_y + width, :] = HI[...]
            M[:, lo:hi, side - width : side, :] = LO[...]
        else:
            M[lo:hi, own_y : own_y + width, :] = HI[...]
            M[lo:hi, side - width : side, :] = LO[...]

    def lane_of(count):
        return lax.broadcasted_iota(jnp.int32, (count, nz), 1)

    def roll(v, shift, axis):
        return pltpu.roll(v, shift % v.shape[axis], axis)

    shape = (own_y, own_y)
    diagonal = lax.broadcasted_iota(jnp.int32, shape, 0) == lax.broadcasted_iota(jnp.int32, shape, 1)
    lane16 = lane_of(own_y)
    loads[3].wait()
    loads[4].wait()
    kinds = land[...]
    ground = jnp.zeros(kinds.shape, F32)
    for kind in range(coeff.shape[0]):
        ground = jnp.where(kinds == kind, coeff[kind], ground)
    loads[2].wait()
    for x in range(own_x):
        column = jnp.sum(jnp.where(diagonal, ground[x : x + 1, :], 0.0), axis=1, keepdims=True)
        low = jnp.where(lane16 == 0, column, 0.0)
        D[OFF + x, 0:own_y, :] = 2.0 * turb[x].astype(F32) + low
    loads[0].wait()
    loads[1].wait()
    pl.semaphore_wait(barrier, len(close))
    w_copies = send_y(W, WLO, WHI, WSL, WSH, 3, True) + send_x(W, 3, True)
    d_copies = send_y(D, DLO, DHI, DSL, DSH, 1) + send_x(D, 1)
    p_copies = send_y(PA, PLO, PHI, PSL, PSH, 3) + send_x(PA, 3)
    finish(w_copies)
    place(W, WLO, WHI, 3, True)
    finish(d_copies)
    place(D, DLO, DHI, 1)

    lane = lane_of(side)
    first, last = lane == 0, lane == nz - 1

    def up0(v):
        return jnp.where(last, 0.0, roll(v, -1, 1))

    def down0(v):
        return jnp.where(first, 0.0, roll(v, 1, 1))

    def stress_row(r):
        v = [W[a, r] for a in range(3)]
        gx = [0.5 * (W[a, r + 1] - W[a, r - 1]) for a in range(3)]
        gy = [0.5 * (roll(v[a], -1, 0) - roll(v[a], 1, 0)) for a in range(3)]
        gz = [up0(v[a]) - down0(v[a]) for a in range(3)]
        e01, e02, e12 = gx[1] + gy[0], gx[2] + gz[0], gy[2] + gz[1]
        q = 2.0 * (gx[0] * gx[0] + gy[1] * gy[1] + gz[2] * gz[2]) + e01 * e01 + e02 * e02 + e12 * e12
        visc = 0.03 * jnp.sqrt(q)
        twice = visc + visc
        t00, t11, t22 = twice * gx[0], twice * gy[1], twice * gz[2]
        t01, t02, t12 = visc * e01, visc * e02, visc * e12
        flat = v[0] * v[0] + v[1] * v[1]
        ghost = 0.03 * jnp.sqrt(2.0 * v[2] * v[2] + flat)
        ghosts = [ghost * v[0], ghost * v[1], (ghost + ghost) * v[2]]
        out = [(T, (0, r), t00), (T, (1, r), t01), (T, (2, r), t02)]
        drag = D[r] * jnp.sqrt(flat)
        for a, (ty, tz) in enumerate(((t01, t02), (t11, t12), (t12, t22))):
            change = 0.5 * (roll(ty, -1, 0) - roll(ty, 1, 0))
            change += jnp.where(last, -ghosts[a], roll(tz, -1, 1)) - jnp.where(first, ghosts[a], roll(tz, 1, 1))
            change -= v[0] * gx[a] + v[1] * gy[a] + v[2] * gz[a]
            if a < 2:
                change -= drag * v[a]
            if a == 0:
                change += 1.0
            out.append((S, (a, r), v[a] + STEP * change))
        return out

    loop(1, rows - 1, stress_row, G_STRESS)

    def star_row(r):
        return [
            (S, (a, r), S[a, r] + (0.5 * STEP) * (T[a, r + 1] - T[a, r - 1])) for a in range(3)
        ]

    loop(2, rows - 2, star_row, G_FINE)

    def source_row(r):
        s1, s2 = S[1, r], S[2, r]
        flat = 0.5 * (S[0, r + 1] - S[0, r - 1] + roll(s1, -1, 0) - roll(s1, 1, 0))
        return [(F, r, (flat + up0(s2) - down0(s2)) / STEP)]

    loop(OFF, OFF + own_x, source_row, G_FINE)
    f_copies = send_y(F, FLO, FHI, FSL, FSH, 2) + send_x(F, 2)
    finish(p_copies)
    place(PA, PLO, PHI, 3)
    finish(f_copies)
    place(F, FLO, FHI, 2)

    def stencil(src, r, sy, sz):
        p = src[r]
        lanes = lane_of(p.shape[0])
        z = jnp.where(lanes >= nz - sz, p, roll(p, -sz, 1)) + jnp.where(lanes < sz, p, roll(p, sz, 1))
        s = src[r + 1] + src[r - 1] + roll(p, -sy, 0) + roll(p, sy, 0)
        return p, s + 4.0 * z

    def sweep(src, dst, f, low, high, sy, sz, group=64):
        def body(r):
            p, around = stencil(src, r, sy, sz)
            return [(dst, r, KEEP * p + WEIGHT * (around - f[r]))]

        loop(low, high, body, min(group, high - low))

    def residual(src, f, r, sy, sz):
        p, around = stencil(src, r, sy, sz)
        return f[r] - (around - 12.0 * p)

    def pair(v, stride, axis):
        at = lax.broadcasted_iota(jnp.int32, v.shape, axis)
        even = (at // stride) % 2 == 0
        return v + jnp.where(even, roll(v, -stride, axis), roll(v, stride, axis))

    def spread(v, stride, bit):
        at = (lane_of(v.shape[0]) // stride) % 2
        return jnp.where(at == bit, v, roll(v, stride if bit == 0 else -stride, 1))

    sweep(PA, PB, F, 1, rows - 1, 1, 1, G_FINE)
    sweep(PB, PA, F, 2, rows - 2, 1, 1, G_FINE)
    PC[OFF : OFF + own_x, 0:own_y, :] = PA[OFF : OFF + own_x, 0:own_y, :]

    half = own_x // 2
    y1 = own_y // 2

    def fine_residual(i):
        r = OFF + 2 * i
        v = residual(PA, F, r, 1, 1) + residual(PA, F, r + 1, 1, 1)
        return [(tmp, i, pair(v[0:own_y], 1, 1))]

    loop(0, half, fine_residual, 2)
    packed = half // 2
    lane8 = lane_of(y1)
    for i in range(packed):
        parts = []
        for x in (2 * i, 2 * i + 1):
            parts.append(0.5 * (tmp[x, pl.ds(0, y1, 2), :] + tmp[x, pl.ds(1, y1, 2), :]))
        G1[0, 3 + i] = jnp.where(lane8 % 2 == 0, parts[0], parts[1])
    g_copies = []
    for dx in (1, -1, 0):
        for dy in range(ny):
            if dx == 0 and dy == 0:
                continue
            if dx == 0:
                src, dst = pl.ds(3, packed), pl.ds(3, packed)
            elif dx == 1:
                src, dst = pl.ds(packed, 3), pl.ds(0, 3)
            else:
                src, dst = pl.ds(3, 3), pl.ds(3 + packed, 3)
            g_copies.append(remote(G1.at[0, src], G1.at[(ny - dy) % ny, dst], device(dx, dy)))
    c_copies = send_y(PC, CLO, CHI, CSL, CSH, 3) + send_x(PC, 3)
    finish(g_copies)
    rows1 = 2 * (packed + 6)
    for k in range(ny):
        for j in range(packed + 6):
            v = G1[k, j]
            for bit in (0, 1):
                f = spread(v, 1, bit)
                F1[2 * j + bit, k * y1 : (k + 1) * y1, :] = f
                P1A[2 * j + bit, k * y1 : (k + 1) * y1, :] = -WEIGHT * f
    sweep(P1A, P1B, F1, 1, rows1 - 1, 1, 2)
    quarter = half // 2
    y2 = ny * y1 // 2
    lane2 = lane_of(y2)
    gathered = None
    for i in range(quarter):
        r = 6 + 2 * i
        tmp2[i] = pair(residual(P1B, F1, r, 1, 2) + residual(P1B, F1, r + 1, 1, 2), 2, 1)
        v = 0.5 * (tmp2[i, pl.ds(0, y2, 2), :] + tmp2[i, pl.ds(1, y2, 2), :])
        gathered = v if gathered is None else jnp.where(lane2 % 4 == i, v, gathered)
    G2[REACH] = gathered
    finish([remote(G2.at[REACH], G2.at[REACH - dx], device(dx, 0)) for dx, dy in friends if dy == 0])
    for s in range(2 * REACH + 1):
        v = G2[s]
        for b0 in (0, 1):
            u = spread(v, 1, b0)
            for b1 in (0, 1):
                f = spread(u, 2, b1)
                F2[4 * s + 2 * b1 + b0] = f
                P2A[4 * s + 2 * b1 + b0] = -WEIGHT * f
    rows2 = 4 * (2 * REACH + 1)
    sweep(P2A, P2B, F2, 1, rows2 - 1, 1, 4)

    def coarse_source(i):
        v = residual(P2B, F2, 2 * i, 1, 4) + residual(P2B, F2, 2 * i + 1, 1, 4)
        f = 0.5 * pair(pair(v, 4, 1), 1, 0)
        return [(F3, i, f), (P3A, i, -WEIGHT * f)]

    loop(1, rows2 // 2 - 1, coarse_source, rows2 // 2 - 2)
    sweep(P3A, P3B, F3, 2, 16, 2, 8)
    sweep(P3B, P3A, F3, 3, 15, 2, 8)
    sweep(P3A, P3B, F3, 4, 14, 2, 8)

    def line_row(r):
        mean = jnp.mean(residual(P3B, F3, r, 2, 8), axis=0, keepdims=True)
        v = P3B[r] - WEIGHT * mean
        return [(P2B, x, P2B[x] + v) for x in (2 * r, 2 * r + 1)]

    loop(6, 12, line_row, 6)
    sweep(P2B, P2A, F2, 13, 23, 1, 4)

    def second_row(m):
        p, around = stencil(P2A, m, 1, 4)
        v = KEEP * p + WEIGHT * (around - F2[m])
        E1[m - 14, pl.ds(0, y2, 2), :] = v
        E1[m - 14, pl.ds(1, y2, 2), :] = v
        e = E1[m - 14]
        r = 2 * (m - 13)
        P1B[r] = P1B[r] + e
        P1B[r + 1] = P1B[r + 1] + e

    for m in range(14, 22):
        second_row(m)
    sweep(P1B, P1A, F1, 3, 17, 1, 2)
    sweep(P1A, P1B, F1, 4, 16, 1, 2)
    finish(c_copies)
    place(PC, CLO, CHI, 3)
    full1 = ny * y1
    for m in range(4, 16):
        e = m - 4
        for shift in (0, 1):
            E0[e, pl.ds(shift, y1, 2), :] = P1B[m, 0:y1, :]
            E0[e, pl.ds(own_y + shift, 2, 2), :] = P1B[m, y1 : y1 + 2, :]
            E0[e, pl.ds(own_y + 4 + shift, 2, 2), :] = P1B[m, full1 - 2 : full1, :]
        for r in (2 * m - 9, 2 * m - 8):
            if 0 <= r < rows:
                PC[r] = PC[r] + E0[e]
    sweep(PC, PA, F, 1, rows - 1, 1, 1, G_FINE)
    sweep(PA, PB, F, 2, rows - 2, 1, 1, G_FINE)

    def out_row(x):
        r = OFF + x
        p = PB[r]
        out = [(pre_out, x, p[0:own_y])]
        gx = (0.5 * STEP) * (PB[r + 1] - PB[r - 1])
        gy = (0.5 * STEP) * (roll(p, -1, 0) - roll(p, 1, 0))
        gz = STEP * (jnp.where(last, p, roll(p, -1, 1)) - jnp.where(first, p, roll(p, 1, 1)))
        for a, g in enumerate((gx, gy, gz)):
            out.append((vel_out, (a, x), (S[a, r] - g)[0:own_y]))
        return out

    loop(0, own_x, out_row, 2)


def per_device(nx, ny, velocity, pressure, land_type, turbine_cells, surface_drag):
    _, own_x, own_y, nz = velocity.shape
    side = (own_y // 8 + 1) * 8
    rows = own_x + 2 * OFF
    window = pltpu.VMEM((rows, side, nz), F32)

    def rims(width, *lead):
        rim = pltpu.VMEM((*lead, own_x + 2 * width, width, nz), F32)
        stage = pltpu.VMEM((*lead, own_x, width, nz), F32)
        return [rim, rim, stage, stage]

    three = pltpu.VMEM((3, rows, side, nz), F32)
    half, quarter = own_x // 2, own_x // 4
    y1 = own_y // 2
    full1, full2 = ny * y1, ny * y1 // 2
    packed = half // 2
    level1 = pltpu.VMEM((2 * (packed + 6), full1, nz), F32)
    rows2 = quarter * (2 * REACH + 1)
    level2 = pltpu.VMEM((rows2, full2, nz), F32)
    level3 = pltpu.VMEM((rows2 // 2, full2, nz), F32)
    count = 5 * 8 + 3 * ny - 1 + 2 * REACH
    scratch = [three] + rims(3, 3) + [window] + rims(1) + [window] + rims(3)
    scratch += [window, window] + rims(3) + [window] + rims(2) + [three, three]
    scratch += [
        pltpu.VMEM((half, own_y, nz), F32),
        pltpu.VMEM((quarter, full1, nz), F32),
        pltpu.VMEM((own_x, own_y, nz), jnp.int32),
        pltpu.VMEM(land_type.shape, jnp.int32),
        pltpu.SMEM(surface_drag.shape, F32),
        pltpu.VMEM((ny, packed + 6, y1, nz), F32),
        level1, level1, level1,
        pltpu.VMEM((2 * REACH + 1, full2, nz), F32),
        level2, level2, level2, level3, level3, level3,
        pltpu.VMEM((8, full1, nz), F32),
        pltpu.VMEM((12, side, nz), F32),
        pltpu.SemaphoreType.DMA((5,)),
        pltpu.SemaphoreType.DMA((count,)),
        pltpu.SemaphoreType.DMA((count,)),
    ]
    inside = pl.BlockSpec(memory_space=pltpu.VMEM)
    return tuple(
        pl.pallas_call(
            functools.partial(kernel, nx, ny),
            out_shape=(
                jax.ShapeDtypeStruct(velocity.shape, F32),
                jax.ShapeDtypeStruct(pressure.shape, F32),
            ),
            in_specs=[pl.BlockSpec(memory_space=pltpu.HBM)] * 5,
            out_specs=(inside, inside),
            scratch_shapes=scratch,
            compiler_params=pltpu.CompilerParams(
                collective_id=0, has_side_effects=True, vmem_limit_bytes=VMEM_LIMIT
            ),
        )(velocity, pressure, turbine_cells, land_type, surface_drag)
    )


def solution(mesh):
    in_specs = (
        P(None, "gx", "gy", None),
        P("gx", "gy", None),
        P("gx", "gy"),
        P("gx", "gy", None),
        P(),
    )
    out_specs = (P(None, "gx", "gy", None), P("gx", "gy", None))
    body = functools.partial(per_device, mesh.shape["gx"], mesh.shape["gy"])
    return jax.shard_map(
        body, mesh=mesh, in_specs=in_specs, out_specs=out_specs, check_vma=False
    )
```

```python
import functools

import jax
import jax.numpy as jnp
from jax import lax
from jax.experimental import pallas as pl
from jax.experimental.pallas import tpu as pltpu
from jax.sharding import PartitionSpec as P

MESH = pl.DeviceIdType.MESH
F32 = jnp.float32
STEP = 0.1
WEIGHT = 0.8 / 12.0
KEEP = 0.2
OFF = 3
G_STRESS = 4
G_FINE = 8
VMEM_LIMIT = 60 * 1024 * 1024
REACH = 4


def loop(low, high, body, group):
    def run(indices):
        found = [store for index in indices for store in body(index)]
        for ref, at, value in found:
            ref[at] = value

    whole = (high - low) // group
    if whole == 1:
        run(range(low, low + group))
    elif whole > 1:

        def step(index, carry):
            run([low + index * group + k for k in range(group)])
            return carry

        lax.fori_loop(0, whole, step, 0)
    if low + whole * group < high:
        run(range(low + whole * group, high))


def kernel(
    nx, ny, vel_in, pre_in, turb_in, land_in, coeff_in, vel_out, pre_out,
    W, WLO, WHI, WSL, WSH, D, DLO, DHI, DSL, DSH, PA, PLO, PHI, PSL, PSH,
    PB, PC, CLO, CHI, CSL, CSH, F, FLO, FHI, FSL, FSH, T, S, tmp, tmp2, turb, land, coeff,
    G1, F1, P1A, P1B, G2, F2, P2A, P2B, F3, P3A, P3B, E1, E0,
    load_sem, send_sem, recv_sem,
):
    me_x, me_y = lax.axis_index("gx"), lax.axis_index("gy")
    own_x, own_y, nz = pre_out.shape
    side = (own_y // 8 + 1) * 8
    rows = own_x + 2 * OFF

    loads = [
        pltpu.make_async_copy(vel_in, W.at[:, OFF : OFF + own_x, 0:own_y], load_sem.at[0]),
        pltpu.make_async_copy(pre_in, PA.at[OFF : OFF + own_x, 0:own_y], load_sem.at[1]),
        pltpu.make_async_copy(turb_in, turb, load_sem.at[2]),
        pltpu.make_async_copy(land_in, land, load_sem.at[3]),
        pltpu.make_async_copy(coeff_in, coeff, load_sem.at[4]),
    ]
    for load in loads:
        load.start()

    def device(dx, dy):
        return (lax.rem(me_x + dx + nx, nx), lax.rem(me_y + dy + ny, ny))

    friends = [(dx, 0) for dx in range(-REACH, REACH + 1) if dx != 0]
    friends += [(dx, dy) for dx in (-1, 0, 1) for dy in range(1, ny)]
    close = [(dx, dy) for dx, dy in friends if abs(dx) < 2]
    barrier = pltpu.get_barrier_semaphore()
    for dx, dy in close:
        pl.semaphore_signal(barrier, inc=1, device_id=device(dx, dy), device_id_type=MESH)

    used = [0]

    def remote(src, dst, where):
        slot = used[0]
        used[0] += 1
        copy = pltpu.make_async_remote_copy(
            src_ref=src, dst_ref=dst, send_sem=send_sem.at[slot], recv_sem=recv_sem.at[slot],
            device_id=where, device_id_type=MESH,
        )
        copy.start()
        return copy

    def spans(dx, width, base):
        if dx == 0:
            return pl.ds(base, own_x), pl.ds(base, own_x)
        if dx == 1:
            return pl.ds(base + own_x - width, width), pl.ds(base - width, width)
        return pl.ds(base, width), pl.ds(base + own_x, width)

    def pick(ref, span, lead):
        return ref.at[:, span] if lead else ref.at[span]

    def send_x(M, width, lead=False):
        copies = []
        for dx in (1, -1):
            src, dst = spans(dx, width, OFF)
            a = M.at[:, src, 0:own_y] if lead else M.at[src, 0:own_y]
            b = M.at[:, dst, 0:own_y] if lead else M.at[dst, 0:own_y]
            copies.append(remote(a, b, device(dx, 0)))
        return copies

    def send_y(M, LO, HI, SL, SH, width, lead=False):
        if lead:
            SL[...] = M[:, OFF : OFF + own_x, own_y - width : own_y, :]
            SH[...] = M[:, OFF : OFF + own_x, 0:width, :]
        else:
            SL[...] = M[OFF : OFF + own_x, own_y - width : own_y, :]
            SH[...] = M[OFF : OFF + own_x, 0:width, :]
        copies = []
        for dx in (0, 1, -1):
            src, dst = spans(dx, width, width)
            if dx == 0:
                src = pl.ds(0, own_x)
            elif dx == 1:
                src = pl.ds(own_x - width, width)
            else:
                src = pl.ds(0, width)
            copies.append(remote(pick(SL, src, lead), pick(LO, dst, lead), device(dx, 1)))
            copies.append(remote(pick(SH, src, lead), pick(HI, dst, lead), device(dx, -1)))
        return copies

    def finish(copies):
        for copy in copies:
            copy.wait()

    def place(M, LO, HI, width, lead=False):
        lo, hi = OFF - width, OFF + own_x + width
        if lead:
            M[:, lo:hi, own_y : own_y + width, :] = HI[...]
            M[:, lo:hi, side - width : side, :] = LO[...]
        else:
            M[lo:hi, own_y : own_y + width, :] = HI[...]
            M[lo:hi, side - width : side, :] = LO[...]

    def lane_of(count):
        return lax.broadcasted_iota(jnp.int32, (count, nz), 1)

    def roll(v, shift, axis):
        return pltpu.roll(v, shift % v.shape[axis], axis)

    shape = (own_y, own_y)
    diagonal = lax.broadcasted_iota(jnp.int32, shape, 0) == lax.broadcasted_iota(jnp.int32, shape, 1)
    lane16 = lane_of(own_y)
    loads[3].wait()
    loads[4].wait()
    kinds = land[...]
    ground = jnp.zeros(kinds.shape, F32)
    for kind in range(coeff.shape[0]):
        ground = jnp.where(kinds == kind, coeff[kind], ground)
    loads[2].wait()
    for x in range(own_x):
        column = jnp.sum(jnp.where(diagonal, ground[x : x + 1, :], 0.0), axis=1, keepdims=True)
        low = jnp.where(lane16 == 0, column, 0.0)
        D[OFF + x, 0:own_y, :] = 2.0 * turb[x].astype(F32) + low
    loads[0].wait()
    loads[1].wait()
    pl.semaphore_wait(barrier, len(close))
    w_copies = send_y(W, WLO, WHI, WSL, WSH, 3, True) + send_x(W, 3, True)
    d_copies = send_y(D, DLO, DHI, DSL, DSH, 1) + send_x(D, 1)
    p_copies = send_y(PA, PLO, PHI, PSL, PSH, 3) + send_x(PA, 3)
    finish(w_copies)
    place(W, WLO, WHI, 3, True)
    finish(d_copies)
    place(D, DLO, DHI, 1)

    lane = lane_of(side)
    first, last = lane == 0, lane == nz - 1

    def up0(v):
        return jnp.where(last, 0.0, roll(v, -1, 1))

    def down0(v):
        return jnp.where(first, 0.0, roll(v, 1, 1))

    def stress_row(r):
        v = [W[a, r] for a in range(3)]
        gx = [0.5 * (W[a, r + 1] - W[a, r - 1]) for a in range(3)]
        gy = [0.5 * (roll(v[a], -1, 0) - roll(v[a], 1, 0)) for a in range(3)]
        gz = [up0(v[a]) - down0(v[a]) for a in range(3)]
        e01, e02, e12 = gx[1] + gy[0], gx[2] + gz[0], gy[2] + gz[1]
        q = 2.0 * (gx[0] * gx[0] + gy[1] * gy[1] + gz[2] * gz[2]) + e01 * e01 + e02 * e02 + e12 * e12
        visc = 0.03 * jnp.sqrt(q)
        twice = visc + visc
        t00, t11, t22 = twice * gx[0], twice * gy[1], twice * gz[2]
        t01, t02, t12 = visc * e01, visc * e02, visc * e12
        flat = v[0] * v[0] + v[1] * v[1]
        ghost = 0.03 * jnp.sqrt(2.0 * v[2] * v[2] + flat)
        ghosts = [ghost * v[0], ghost * v[1], (ghost + ghost) * v[2]]
        out = [(T, (0, r), t00), (T, (1, r), t01), (T, (2, r), t02)]
        drag = D[r] * jnp.sqrt(flat)
        for a, (ty, tz) in enumerate(((t01, t02), (t11, t12), (t12, t22))):
            change = 0.5 * (roll(ty, -1, 0) - roll(ty, 1, 0))
            change += jnp.where(last, -ghosts[a], roll(tz, -1, 1)) - jnp.where(first, ghosts[a], roll(tz, 1, 1))
            change -= v[0] * gx[a] + v[1] * gy[a] + v[2] * gz[a]
            if a < 2:
                change -= drag * v[a]
            if a == 0:
                change += 1.0
            out.append((S, (a, r), v[a] + STEP * change))
        return out

    loop(1, rows - 1, stress_row, G_STRESS)

    def star_row(r):
        return [
            (S, (a, r), S[a, r] + (0.5 * STEP) * (T[a, r + 1] - T[a, r - 1])) for a in range(3)
        ]

    loop(2, rows - 2, star_row, G_FINE)

    def source_row(r):
        s1, s2 = S[1, r], S[2, r]
        flat = 0.5 * (S[0, r + 1] - S[0, r - 1] + roll(s1, -1, 0) - roll(s1, 1, 0))
        return [(F, r, (flat + up0(s2) - down0(s2)) / STEP)]

    loop(OFF, OFF + own_x, source_row, G_FINE)
    f_copies = send_y(F, FLO, FHI, FSL, FSH, 2) + send_x(F, 2)
    finish(p_copies)
    place(PA, PLO, PHI, 3)
    finish(f_copies)
    place(F, FLO, FHI, 2)

    def stencil(src, r, sy, sz):
        p = src[r]
        lanes = lane_of(p.shape[0])
        z = jnp.where(lanes >= nz - sz, p, roll(p, -sz, 1)) + jnp.where(lanes < sz, p, roll(p, sz, 1))
        s = src[r + 1] + src[r - 1] + roll(p, -sy, 0) + roll(p, sy, 0)
        return p, s + 4.0 * z

    def sweep(src, dst, f, low, high, sy, sz, group=64):
        def body(r):
            p, around = stencil(src, r, sy, sz)
            return [(dst, r, KEEP * p + WEIGHT * (around - f[r]))]

        loop(low, high, body, min(group, high - low))

    def residual(src, f, r, sy, sz):
        p, around = stencil(src, r, sy, sz)
        return f[r] - (around - 12.0 * p)

    def pair(v, stride, axis):
        at = lax.broadcasted_iota(jnp.int32, v.shape, axis)
        even = (at // stride) % 2 == 0
        return v + jnp.where(even, roll(v, -stride, axis), roll(v, stride, axis))

    def spread(v, stride, bit):
        at = (lane_of(v.shape[0]) // stride) % 2
        return jnp.where(at == bit, v, roll(v, stride if bit == 0 else -stride, 1))

    sweep(PA, PB, F, 1, rows - 1, 1, 1, G_FINE)
    sweep(PB, PA, F, 2, rows - 2, 1, 1, G_FINE)
    PC[OFF : OFF + own_x, 0:own_y, :] = PA[OFF : OFF + own_x, 0:own_y, :]

    half = own_x // 2
    y1 = own_y // 2

    def fine_residual(i):
        r = OFF + 2 * i
        v = residual(PA, F, r, 1, 1) + residual(PA, F, r + 1, 1, 1)
        return [(tmp, i, pair(v[0:own_y], 1, 1))]

    loop(0, half, fine_residual, 2)
    packed = half // 2
    lane8 = lane_of(y1)
    for i in range(packed):
        parts = []
        for x in (2 * i, 2 * i + 1):
            parts.append(0.5 * (tmp[x, pl.ds(0, y1, 2), :] + tmp[x, pl.ds(1, y1, 2), :]))
        G1[0, 3 + i] = jnp.where(lane8 % 2 == 0, parts[0], parts[1])
    g_copies = []
    for dx in (1, -1, 0):
        for dy in range(ny):
            if dx == 0 and dy == 0:
                continue
            if dx == 0:
                src, dst = pl.ds(3, packed), pl.ds(3, packed)
            elif dx == 1:
                src, dst = pl.ds(packed, 3), pl.ds(0, 3)
            else:
                src, dst = pl.ds(3, 3), pl.ds(3 + packed, 3)
            g_copies.append(remote(G1.at[0, src], G1.at[(ny - dy) % ny, dst], device(dx, dy)))
    c_copies = send_y(PC, CLO, CHI, CSL, CSH, 3) + send_x(PC, 3)
    finish(g_copies)
    rows1 = 2 * (packed + 6)
    for k in range(ny):
        for j in range(packed + 6):
            v = G1[k, j]
            for bit in (0, 1):
                f = spread(v, 1, bit)
                F1[2 * j + bit, k * y1 : (k + 1) * y1, :] = f
                P1A[2 * j + bit, k * y1 : (k + 1) * y1, :] = -WEIGHT * f
    sweep(P1A, P1B, F1, 1, rows1 - 1, 1, 2)
    quarter = half // 2
    y2 = ny * y1 // 2
    lane2 = lane_of(y2)
    gathered = None
    for i in range(quarter):
        r = 6 + 2 * i
        tmp2[i] = pair(residual(P1B, F1, r, 1, 2) + residual(P1B, F1, r + 1, 1, 2), 2, 1)
        v = 0.5 * (tmp2[i, pl.ds(0, y2, 2), :] + tmp2[i, pl.ds(1, y2, 2), :])
        gathered = v if gathered is None else jnp.where(lane2 % 4 == i, v, gathered)
    G2[REACH] = gathered
    finish([remote(G2.at[REACH], G2.at[REACH - dx], device(dx, 0)) for dx, dy in friends if dy == 0])
    for s in range(2 * REACH + 1):
        v = G2[s]
        for b0 in (0, 1):
            u = spread(v, 1, b0)
            for b1 in (0, 1):
                f = spread(u, 2, b1)
                F2[4 * s + 2 * b1 + b0] = f
                P2A[4 * s + 2 * b1 + b0] = -WEIGHT * f
    rows2 = 4 * (2 * REACH + 1)
    sweep(P2A, P2B, F2, 1, rows2 - 1, 1, 4)

    def coarse_source(i):
        v = residual(P2B, F2, 2 * i, 1, 4) + residual(P2B, F2, 2 * i + 1, 1, 4)
        f = 0.5 * pair(pair(v, 4, 1), 1, 0)
        return [(F3, i, f), (P3A, i, -WEIGHT * f)]

    loop(1, rows2 // 2 - 1, coarse_source, rows2 // 2 - 2)
    sweep(P3A, P3B, F3, 2, 16, 2, 8)
    sweep(P3B, P3A, F3, 3, 15, 2, 8)
    sweep(P3A, P3B, F3, 4, 14, 2, 8)

    def line_row(r):
        mean = jnp.mean(residual(P3B, F3, r, 2, 8), axis=0, keepdims=True)
        v = P3B[r] - WEIGHT * mean
        return [(P2B, x, P2B[x] + v) for x in (2 * r, 2 * r + 1)]

    loop(6, 12, line_row, 6)
    sweep(P2B, P2A, F2, 13, 23, 1, 4)

    def second_row(m):
        p, around = stencil(P2A, m, 1, 4)
        v = KEEP * p + WEIGHT * (around - F2[m])
        E1[m - 14, pl.ds(0, y2, 2), :] = v
        E1[m - 14, pl.ds(1, y2, 2), :] = v
        e = E1[m - 14]
        r = 2 * (m - 13)
        P1B[r] = P1B[r] + e
        P1B[r + 1] = P1B[r + 1] + e

    for m in range(14, 22):
        second_row(m)
    sweep(P1B, P1A, F1, 3, 17, 1, 2)
    sweep(P1A, P1B, F1, 4, 16, 1, 2)
    finish(c_copies)
    place(PC, CLO, CHI, 3)
    full1 = ny * y1
    for m in range(4, 16):
        e = m - 4
        for shift in (0, 1):
            E0[e, pl.ds(shift, y1, 2), :] = P1B[m, 0:y1, :]
            E0[e, pl.ds(own_y + shift, 2, 2), :] = P1B[m, y1 : y1 + 2, :]
            E0[e, pl.ds(own_y + 4 + shift, 2, 2), :] = P1B[m, full1 - 2 : full1, :]
        for r in (2 * m - 9, 2 * m - 8):
            if 0 <= r < rows:
                PC[r] = PC[r] + E0[e]
    sweep(PC, PA, F, 1, rows - 1, 1, 1, G_FINE)
    sweep(PA, PB, F, 2, rows - 2, 1, 1, G_FINE)

    def out_row(x):
        r = OFF + x
        p = PB[r]
        out = [(pre_out, x, p[0:own_y])]
        gx = (0.5 * STEP) * (PB[r + 1] - PB[r - 1])
        gy = (0.5 * STEP) * (roll(p, -1, 0) - roll(p, 1, 0))
        gz = STEP * (jnp.where(last, p, roll(p, -1, 1)) - jnp.where(first, p, roll(p, 1, 1)))
        for a, g in enumerate((gx, gy, gz)):
            out.append((vel_out, (a, x), (S[a, r] - g)[0:own_y]))
        return out

    loop(0, own_x, out_row, 2)


def per_device(nx, ny, velocity, pressure, land_type, turbine_cells, surface_drag):
    _, own_x, own_y, nz = velocity.shape
    side = (own_y // 8 + 1) * 8
    rows = own_x + 2 * OFF
    window = pltpu.VMEM((rows, side, nz), F32)

    def rims(width, *lead):
        rim = pltpu.VMEM((*lead, own_x + 2 * width, width, nz), F32)
        stage = pltpu.VMEM((*lead, own_x, width, nz), F32)
        return [rim, rim, stage, stage]

    three = pltpu.VMEM((3, rows, side, nz), F32)
    half, quarter = own_x // 2, own_x // 4
    y1 = own_y // 2
    full1, full2 = ny * y1, ny * y1 // 2
    packed = half // 2
    level1 = pltpu.VMEM((2 * (packed + 6), full1, nz), F32)
    rows2 = quarter * (2 * REACH + 1)
    level2 = pltpu.VMEM((rows2, full2, nz), F32)
    level3 = pltpu.VMEM((rows2 // 2, full2, nz), F32)
    count = 5 * 8 + 3 * ny - 1 + 2 * REACH
    scratch = [three] + rims(3, 3) + [window] + rims(1) + [window] + rims(3)
    scratch += [window, window] + rims(3) + [window] + rims(2) + [three, three]
    scratch += [
        pltpu.VMEM((half, own_y, nz), F32),
        pltpu.VMEM((quarter, full1, nz), F32),
        pltpu.VMEM((own_x, own_y, nz), jnp.int32),
        pltpu.VMEM(land_type.shape, jnp.int32),
        pltpu.SMEM(surface_drag.shape, F32),
        pltpu.VMEM((ny, packed + 6, y1, nz), F32),
        level1, level1, level1,
        pltpu.VMEM((2 * REACH + 1, full2, nz), F32),
        level2, level2, level2, level3, level3, level3,
        pltpu.VMEM((8, full1, nz), F32),
        pltpu.VMEM((12, side, nz), F32),
        pltpu.SemaphoreType.DMA((5,)),
        pltpu.SemaphoreType.DMA((count,)),
        pltpu.SemaphoreType.DMA((count,)),
    ]
    inside = pl.BlockSpec(memory_space=pltpu.VMEM)
    moved = tuple(
        pl.pallas_call(
            functools.partial(kernel, nx, ny),
            out_shape=(
                jax.ShapeDtypeStruct(velocity.shape, F32),
                jax.ShapeDtypeStruct(pressure.shape, F32),
            ),
            in_specs=[pl.BlockSpec(memory_space=pltpu.HBM)] * 5,
            out_specs=(inside, inside),
            scratch_shapes=scratch,
            compiler_params=pltpu.CompilerParams(
                collective_id=0, has_side_effects=True, vmem_limit_bytes=VMEM_LIMIT
            ),
        )(velocity, pressure, turbine_cells, land_type, surface_drag)
    )
    parts = 2
    vel_block = pl.BlockSpec((3, own_x // parts, own_y, nz), lambda i: (0, i, 0, 0))
    pre_block = pl.BlockSpec((own_x // parts, own_y, nz), lambda i: (i, 0, 0))
    return pl.pallas_call(
        hand_over,
        grid=(parts,),
        out_shape=(
            jax.ShapeDtypeStruct(velocity.shape, F32),
            jax.ShapeDtypeStruct(pressure.shape, F32),
        ),
        in_specs=[vel_block, pre_block],
        out_specs=(vel_block, pre_block),
    )(*moved)


def hand_over(vel_in, pre_in, vel_out, pre_out):
    vel_out[...] = vel_in[...]
    pre_out[...] = pre_in[...]


def solution(mesh):
    in_specs = (
        P(None, "gx", "gy", None),
        P("gx", "gy", None),
        P("gx", "gy"),
        P("gx", "gy", None),
        P(),
    )
    out_specs = (P(None, "gx", "gy", None), P("gx", "gy", None))
    body = functools.partial(per_device, mesh.shape["gx"], mesh.shape["gy"])
    return jax.shard_map(
        body, mesh=mesh, in_specs=in_specs, out_specs=out_specs, check_vma=False
    )
```
